32 devices in a mesh: frame: 4 (over y, x), row: 8 (over z, core).
Axes of the slice: x: 2, y: 2, z: 4, core: 2. Of those that a mesh axis runs over, the one named last changes fastest.
Arguments:
- residual_in: bfloat16 [4, 8, 64, 768], P('frame', 'row'), may hold values from -6 to 6
- q_spatial: bfloat16 [4, 8, 64, 768], P('frame', 'row'), may hold values from -250 to 250
- k_spatial: bfloat16 [4, 8, 64, 768], P('frame', 'row'), may hold values from -250 to 250
- v_spatial: bfloat16 [4, 8, 64, 768], P('frame', 'row'), may hold values from -6 to 6
- q_temporal: bfloat16 [4, 8, 64, 768], P('frame', 'row'), may hold values from -250 to 250
- k_temporal: bfloat16 [4, 8, 64, 768], P('frame', 'row'), may hold values from -250 to 250
- conv_weight: float32 [3, 3, 768], replicated, may hold values from -2 to 2
- conv_bias: float32 [768], replicated, may hold values from -3 to 3
Outputs:
- spatial_out: bfloat16 [4, 8, 64, 768], P('frame', 'row')
- block_out: bfloat16 [4, 8, 64, 768], P('frame', 'row')
The draws below stay inside these ranges and needn't reach their ends.
All inputs are finite; a program needn't handle non-finite values.
Results may differ from the reference program's by a relative error of at most 0.0061.
Values may be sent and summed in bfloat16 or wider, within the bound.
A program may use at most 64 MiB of HBM per device.

```python
import math
import jax
import jax.numpy as jnp
from jax import lax

HEADS = 12
HEAD_DIM = 64
C = 768
WIDE = 64
HEIGHT = 8
FRAMES = 4


def base_pair(key, first_salt, second_salt):
    shape = (FRAMES, HEIGHT * WIDE, HEADS * HEAD_DIM)
    queries = jnp.clip(jax.random.normal(jax.random.fold_in(key, first_salt), shape, jnp.float32) * 1.7, -6.8, 6.8)
    keys = jnp.clip(jax.random.normal(jax.random.fold_in(key, second_salt), shape, jnp.float32) * 1.7, -6.8, 6.8)
    return (queries, keys)


def spatial_pair(key):
    queries, keys = base_pair(key, 11, 12)
    return (queries.reshape(FRAMES, HEIGHT, WIDE, HEADS * HEAD_DIM), keys.reshape(FRAMES, HEIGHT, WIDE, HEADS * HEAD_DIM))


def temporal_pair(key):
    queries, keys = base_pair(key, 21, 22)
    return (queries.reshape(FRAMES, HEIGHT, WIDE, HEADS * HEAD_DIM), keys.reshape(FRAMES, HEIGHT, WIDE, HEADS * HEAD_DIM))


def draw_q_spatial(key, part):
    return spatial_pair(key)[0].astype(jnp.bfloat16)


def draw_k_spatial(key, part):
    return spatial_pair(key)[1].astype(jnp.bfloat16)


def draw_q_temporal(key, part):
    return temporal_pair(key)[0].astype(jnp.bfloat16)


def draw_k_temporal(key, part):
    return temporal_pair(key)[1].astype(jnp.bfloat16)


def block_levels(key, dims, split, smallest, top_value):
    level = 1.0
    for axis_at, parts in split:
        steps = jax.random.uniform(jax.random.fold_in(jax.random.fold_in(key, 6), axis_at), (parts,), jnp.float32, smallest / len(split), top_value / len(split))
        level = level * jnp.repeat(jnp.exp(steps), dims[axis_at] // parts).reshape((-1,) + (1,) * (len(dims) - 1 - axis_at))
    return level


def bell_draw(key, extent, width, limit, pieces=(), kind=jnp.bfloat16):
    level = block_levels(key, extent, pieces, -0.22, 0.18) if pieces else 1.0
    values = jax.random.normal(key, extent, jnp.float32) * width * level
    return jnp.minimum(jnp.maximum(values, -limit), limit).astype(kind)


def setup_inputs(seed: int = 0) -> dict:
    seeds = jax.random.split(jax.random.key(seed), 9)
    return {
        "residual_in": bell_draw(seeds[0], (FRAMES, HEIGHT, WIDE, C), 1.0, 6.0, ((0, 4), (1, 8))),
        "q_spatial": draw_q_spatial(jax.random.fold_in(seeds[8], 71), 0),
        "k_spatial": draw_k_spatial(jax.random.fold_in(seeds[8], 71), 0),
        "v_spatial": bell_draw(seeds[3], (FRAMES, HEIGHT, WIDE, C), 1.0, 6.0, ((0, 4), (1, 8))),
        "q_temporal": draw_q_temporal(jax.random.fold_in(seeds[8], 71), 0),
        "k_temporal": draw_k_temporal(jax.random.fold_in(seeds[8], 71), 0),
        "conv_weight": bell_draw(seeds[6], (3, 3, C), 0.35, 2.0, (), jnp.float32),
        "conv_bias": bell_draw(seeds[7], (C,), 0.5, 3.0, (), jnp.float32),
    }


def spatial_frame(operands):
    query_rows, key_rows, value_rows = operands
    count = HEIGHT * WIDE
    block = math.gcd(count, 512)
    keys_f = key_rows.astype(jnp.float32).reshape(count, HEADS, HEAD_DIM)
    values_f = value_rows.astype(jnp.float32).reshape(count, HEADS, HEAD_DIM)
    queries_f = query_rows.astype(jnp.float32).reshape(count // block, block, HEADS, HEAD_DIM)

    def one_block(query_block):
        scores = jnp.einsum("thd,khd->htk", query_block, keys_f) * HEAD_DIM ** -0.5
        peak = jnp.max(scores, axis=-1, keepdims=True)
        raised = jnp.exp(scores - peak)
        totals = jnp.sum(raised, axis=-1)
        weights = lax.optimization_barrier(raised.astype(jnp.bfloat16)).astype(jnp.float32)
        blended = jnp.einsum("htk,khd->htd", weights, values_f) / totals[..., None]
        return jnp.transpose(blended, (1, 0, 2)).reshape(block, HEADS * HEAD_DIM)

    return lax.map(one_block, queries_f).reshape(count, HEADS * HEAD_DIM)


def temporal_mix(queries, keys, values):
    shape5 = (FRAMES, HEIGHT, WIDE, HEADS, HEAD_DIM)
    query_f = queries.astype(jnp.float32).reshape(shape5)
    key_f = keys.astype(jnp.float32).reshape(shape5)
    value_f = values.astype(jnp.float32).reshape(shape5)
    scores = jnp.einsum("fywhd,gywhd->ywhfg", query_f, key_f) * HEAD_DIM ** -0.5
    frame_ids = jnp.arange(FRAMES)
    allowed = frame_ids[:, None] >= frame_ids[None, :]
    scores = jnp.where(allowed, scores, -1e30)
    peak = jnp.max(scores, axis=-1, keepdims=True)
    raised = jnp.exp(scores - peak)
    totals = jnp.sum(raised, axis=-1)
    weights = lax.optimization_barrier(raised.astype(jnp.bfloat16)).astype(jnp.float32)
    blended = jnp.einsum("ywhfg,gywhd->fywhd", weights, value_f) / jnp.moveaxis(totals, 3, 0)[..., None]
    return blended.reshape(FRAMES, HEIGHT, WIDE, HEADS * HEAD_DIM)


def reference(residual_in, q_spatial, k_spatial, v_spatial, q_temporal, k_temporal, conv_weight, conv_bias):
    count = HEIGHT * WIDE
    channels = HEADS * HEAD_DIM
    attended = lax.map(spatial_frame, (q_spatial.reshape(FRAMES, count, channels),
                                       k_spatial.reshape(FRAMES, count, channels),
                                       v_spatial.reshape(FRAMES, count, channels)))
    spatial_out = attended.astype(jnp.bfloat16).reshape(FRAMES, HEIGHT, WIDE, channels)
    hidden = (residual_in.astype(jnp.float32) + spatial_out.astype(jnp.float32)).astype(jnp.bfloat16)
    temporal = temporal_mix(q_temporal, k_temporal, hidden).astype(jnp.bfloat16)
    mixed = (hidden.astype(jnp.float32) + temporal.astype(jnp.float32)).astype(jnp.bfloat16)
    padded = jnp.pad(mixed.astype(jnp.float32), ((0, 0), (1, 1), (1, 1), (0, 0)))
    conv = jnp.zeros((FRAMES, HEIGHT, WIDE, channels), jnp.float32) + conv_bias
    for first in range(3):
        for second in range(3):
            conv = conv + conv_weight[first, second] * padded[:, first:first + HEIGHT, second:second + WIDE]
    block_out = (mixed.astype(jnp.float32) + jax.nn.gelu(conv)).astype(jnp.bfloat16)
    return spatial_out, block_out
```

```python
import functools
import math

import jax
import jax.numpy as jnp
from jax import lax
from jax.experimental import pallas as pl
from jax.experimental.pallas import tpu as pltpu
from jax.sharding import PartitionSpec as P

HEAD_DIM = 64
LANES = 2 * HEAD_DIM
SCALE = HEAD_DIM ** (-0.5)
LOG2E = math.log2(math.e)


def block_kernel(
    frames, rows, chunks, tokens,
    res_hbm, q_hbm, k_hbm, v_hbm, qt_hbm, kt_hbm, cw_hbm, cb_hbm,
    so_hbm, bo_hbm,
    kv, qs, rs, qts, ktb, hb, tsc, wts, peak, rden, mixb, sob, bob, cwv, cbv,
    ld_kv, ld_misc, kv_recv, up_send, dn_send, pt_send,
    kt_recv, kt_send, h_recv, h_send, halo_recv, halo_send, out_sem,
):
    me_f = lax.axis_index("frame")
    me_r = lax.axis_index("row")
    chips = rows // 2
    z = me_r // 2
    core = me_r % 2

    def lanes(c):
        return pl.ds(c * LANES, LANES)

    for c in range(chunks):
        pltpu.make_async_copy(k_hbm.at[0, 0, :, lanes(c)], kv.at[me_r, c, 0], ld_kv.at[c]).start()
        pltpu.make_async_copy(v_hbm.at[0, 0, :, lanes(c)], kv.at[me_r, c, 1], ld_kv.at[c]).start()
    for c in range(chunks):
        pltpu.make_async_copy(kt_hbm.at[0, 0, :, lanes(c)], ktb.at[me_f, c], ld_misc.at[0]).start()
    for c in range(chunks):
        pltpu.make_async_copy(qt_hbm.at[0, 0, :, lanes(c)], qts.at[c], ld_misc.at[1]).start()
        pltpu.make_async_copy(q_hbm.at[0, 0, :, lanes(c)], qs.at[c], ld_misc.at[2]).start()
        pltpu.make_async_copy(res_hbm.at[0, 0, :, lanes(c)], rs.at[c], ld_misc.at[3]).start()
    pltpu.make_async_copy(cw_hbm, cwv, ld_misc.at[4]).start()
    pltpu.make_async_copy(cb_hbm, cbv, ld_misc.at[5]).start()

    barrier = pltpu.get_barrier_semaphore()

    def greet(**where):
        pl.semaphore_signal(
            barrier, inc=1, device_id=where, device_id_type=pl.DeviceIdType.MESH
        )

    greet(row=me_r + 1 - 2 * core)

    @pl.when(z > 0)
    def _():
        greet(row=me_r - 2)

    @pl.when(z < chips - 1)
    def _():
        greet(row=me_r + 2)

    across = me_r - 1 + 2 * core
    has_across = jnp.logical_and(across >= 0, across < rows)

    @pl.when(has_across)
    def _():
        greet(row=across)

    @pl.loop(1, frames)
    def _(step):
        greet(frame=(me_f + step) % frames)

    pl.semaphore_wait(
        barrier,
        frames
        + (z > 0).astype(jnp.int32)
        + (z < chips - 1).astype(jnp.int32)
        + has_across.astype(jnp.int32),
    )

    def remote(src, dst, send, recv, **where):
        return pltpu.make_async_remote_copy(
            src_ref=src, dst_ref=dst, send_sem=send, recv_sem=recv,
            device_id=where, device_id_type=pl.DeviceIdType.MESH,
        )

    def kv_copy(chip, of_core, c, send, to_row):
        src = 2 * chip + of_core
        return remote(kv.at[src, c], kv.at[src, c], send, kv_recv.at[src, c], row=to_row)

    def go_up(chip, c):
        return kv_copy(chip, core, c, up_send.at[chip, c], me_r + 2)

    def go_down(chip, c):
        return kv_copy(chip, core, c, dn_send.at[chip, c], me_r - 2)

    def to_partner(chip, c):
        return kv_copy(chip, core, c, pt_send.at[chip, c], me_r + 1 - 2 * core)

    def wait_slot(chip, of_core, c):
        kv_copy(chip, of_core, c, up_send.at[chip, c], me_r + 1 - 2 * core).wait_recv()

    def kt_copy(g, to):
        return remote(ktb.at[g], ktb.at[g], kt_send.at[to], kt_recv.at[g], frame=to)

    def h_copy(g, to, c):
        return remote(hb.at[g, c], hb.at[g, c], h_send.at[to, c], h_recv.at[g, c], frame=to)

    def halo_copy(side, c):
        return remote(
            mixb.at[1, c], mixb.at[2 - 2 * side, c], halo_send.at[side, c],
            halo_recv.at[1 - side, c], row=me_r - 1 + 2 * side,
        )

    for c in range(chunks):
        pltpu.make_async_copy(kv.at[me_r, c], kv.at[me_r, c], ld_kv.at[c]).wait()

        @pl.when(z > 0)
        def _(c=c):
            go_down(z, c).start()

        @pl.when(z < chips - 1)
        def _(c=c):
            go_up(z, c).start()

        to_partner(z, c).start()

    pltpu.make_async_copy(ktb.at[me_f], ktb.at[me_f], ld_misc.at[0]).wait()

    @pl.loop(me_f + 1, frames)
    def _(to):
        kt_copy(me_f, to).start()

    def relay(d, c):
        @pl.when(z - d >= 0)
        def _():
            wait_slot(z - d, core, c)

            @pl.when(z < chips - 1)
            def _():
                go_up(z - d, c).start()

            to_partner(z - d, c).start()

        @pl.when(z + d < chips)
        def _():
            wait_slot(z + d, core, c)

            @pl.when(z > 0)
            def _():
                go_down(z + d, c).start()

            to_partner(z + d, c).start()

    @pl.loop(1, chips - 1)
    def _(d):
        for c in range(chunks):
            relay(d, c)

    pltpu.make_async_copy(qts, qts, ld_misc.at[1]).wait()

    @pl.loop(0, me_f)
    def _(g):
        kt_copy(g, me_f).wait_recv()

    flat = chunks * tokens
    same = (
        (lax.broadcasted_iota(jnp.int32, (2 * LANES, LANES), 0) // HEAD_DIM) % 2
        == lax.broadcasted_iota(jnp.int32, (2 * LANES, LANES), 1) // HEAD_DIM
    )
    spread = jnp.where(same, 1.0, 0.0).astype(jnp.bfloat16)
    peak[...] = jnp.full(peak.shape, -1e30, jnp.float32)

    @pl.loop(0, me_f + 1)
    def _(g):
        product = (
            qts[...].reshape(flat, LANES).astype(jnp.float32)
            * ktb[g].reshape(flat, LANES).astype(jnp.float32)
        )
        high = product.astype(jnp.bfloat16)
        low = (product - high.astype(jnp.float32)).astype(jnp.bfloat16)
        score = jnp.dot(
            jnp.concatenate([high, low], axis=1), spread, preferred_element_type=jnp.float32
        )
        tsc[g] = score
        peak[...] = jnp.maximum(peak[...], score)

    rden[...] = jnp.zeros(rden.shape, jnp.float32)

    @pl.loop(0, me_f + 1)
    def _(g):
        raised = jnp.exp2((tsc[g] - peak[...]) * (SCALE * LOG2E))
        rden[...] += raised
        wts[g] = raised.astype(jnp.bfloat16)

    rden[...] = 1.0 / rden[...]

    pltpu.make_async_copy(qs, qs, ld_misc.at[2]).wait()
    pltpu.make_async_copy(rs, rs, ld_misc.at[3]).wait()

    first_head = lax.broadcasted_iota(jnp.int32, (tokens, LANES), 1) < HEAD_DIM
    keys = rows * tokens

    for c in range(chunks):
        relay(chips - 1, c)

        @pl.loop(0, chips)
        def _(chip, c=c):
            wait_slot(chip, 1 - core, c)

        q = qs[c]
        none = jnp.zeros_like(q)
        q2 = jnp.concatenate(
            [jnp.where(first_head, q, none), jnp.where(first_head, none, q)], axis=0
        )
        scores = lax.dot_general(
            q2, kv[:, c, 0].reshape(keys, LANES), (((1,), (1,)), ((), ())),
            preferred_element_type=jnp.float32,
        )
        top = jnp.max(scores, axis=1, keepdims=True)
        raised = jnp.exp2((scores - top) * (SCALE * LOG2E))
        denom = jnp.sum(raised, axis=1, keepdims=True)
        both = jnp.dot(
            raised.astype(jnp.bfloat16), kv[:, c, 1].reshape(keys, LANES),
            preferred_element_type=jnp.float32,
        ) / denom
        spatial = jnp.where(first_head, both[:tokens], both[tokens:]).astype(jnp.bfloat16)
        sob[c] = spatial
        hb[me_f, c] = (rs[c].astype(jnp.float32) + spatial.astype(jnp.float32)).astype(jnp.bfloat16)

        @pl.loop(me_f + 1, frames)
        def _(to, c=c):
            h_copy(me_f, to, c).start()

        pltpu.make_async_copy(sob.at[c], so_hbm.at[0, 0, :, lanes(c)], out_sem.at[0]).start()

    for c in range(chunks):
        @pl.loop(0, me_f)
        def _(g, c=c):
            h_copy(g, me_f, c).wait_recv()

        here = pl.ds(c * tokens, tokens)

        def add(g, total):
            return total + wts[g, here].astype(jnp.float32) * hb[g, c].astype(jnp.float32)

        total = lax.fori_loop(0, me_f + 1, add, jnp.zeros((tokens, LANES), jnp.float32))
        temporal = (total * rden[here]).astype(jnp.bfloat16)
        mixb[1, c] = (
            hb[me_f, c].astype(jnp.float32) + temporal.astype(jnp.float32)
        ).astype(jnp.bfloat16)

        @pl.when(me_r > 0)
        def _(c=c):
            halo_copy(0, c).start()

        @pl.when(me_r < rows - 1)
        def _(c=c):
            halo_copy(1, c).start()

    pltpu.make_async_copy(cwv, cwv, ld_misc.at[4]).wait()
    pltpu.make_async_copy(cbv, cbv, ld_misc.at[5]).wait()

    @pl.when(me_r == 0)
    def _():
        mixb[0] = jnp.zeros(mixb.shape[1:], mixb.dtype)

    @pl.when(me_r == rows - 1)
    def _():
        mixb[2] = jnp.zeros(mixb.shape[1:], mixb.dtype)

    position = lax.broadcasted_iota(jnp.int32, (tokens, LANES), 0)
    for c in range(chunks):
        @pl.when(me_r > 0)
        def _(c=c):
            remote(
                mixb.at[0, c], mixb.at[0, c], halo_send.at[0, c], halo_recv.at[0, c],
                row=me_r - 1,
            ).wait_recv()

        @pl.when(me_r < rows - 1)
        def _(c=c):
            remote(
                mixb.at[2, c], mixb.at[2, c], halo_send.at[1, c], halo_recv.at[1, c],
                row=me_r + 1,
            ).wait_recv()

        lines = [mixb[a, c].astype(jnp.float32) for a in range(3)]
        taps = [
            sum(cwv[a, pl.ds(b, 1), lanes(c)] * lines[a] for a in range(3)) for b in range(3)
        ]
        left = jnp.where(position == 0, 0.0, pltpu.roll(taps[0], 1, 0))
        right = jnp.where(position == tokens - 1, 0.0, pltpu.roll(taps[2], tokens - 1, 0))
        conv = cbv[pl.ds(c * LANES, LANES)].reshape(1, LANES) + taps[1] + left + right
        inner = math.sqrt(2.0 / math.pi) * (conv + 0.044715 * (conv * conv * conv))
        bob[c] = (lines[1] + 0.5 * conv * (1.0 + jnp.tanh(inner))).astype(jnp.bfloat16)
        pltpu.make_async_copy(bob.at[c], bo_hbm.at[0, 0, :, lanes(c)], out_sem.at[1]).start()

    @pl.loop(0, chips)
    def _(chip):
        for c in range(chunks):
            to_partner(chip, c).wait_send()

            @pl.when(jnp.logical_and(chip <= z, z < chips - 1))
            def _(c=c):
                go_up(chip, c).wait_send()

            @pl.when(jnp.logical_and(chip >= z, z > 0))
            def _(c=c):
                go_down(chip, c).wait_send()

    @pl.loop(me_f + 1, frames)
    def _(to):
        kt_copy(me_f, to).wait_send()
        for c in range(chunks):
            h_copy(me_f, to, c).wait_send()

    for c in range(chunks):
        @pl.when(me_r > 0)
        def _(c=c):
            halo_copy(0, c).wait_send()

        @pl.when(me_r < rows - 1)
        def _(c=c):
            halo_copy(1, c).wait_send()

    pltpu.make_async_copy(sob, sob, out_sem.at[0]).wait()
    pltpu.make_async_copy(bob, bob, out_sem.at[1]).wait()


def on_device(frames, rows, *args):
    block = args[0]
    _, _, tokens, channels = block.shape
    chunks = channels // LANES
    chips = rows // 2
    slab = (chunks, tokens, LANES)
    flat = (chunks * tokens, LANES)
    bf16, f32 = jnp.bfloat16, jnp.float32
    dma = pltpu.SemaphoreType.DMA
    anywhere = pl.BlockSpec(memory_space=pl.ANY)
    return pl.pallas_call(
        functools.partial(block_kernel, frames, rows, chunks, tokens),
        out_shape=(jax.ShapeDtypeStruct(block.shape, bf16),) * 2,
        in_specs=[anywhere] * 8,
        out_specs=(anywhere, anywhere),
        scratch_shapes=[
            pltpu.VMEM((rows, chunks, 2, tokens, LANES), bf16),
            pltpu.VMEM(slab, bf16),
            pltpu.VMEM(slab, bf16),
            pltpu.VMEM(slab, bf16),
            pltpu.VMEM((frames,) + slab, bf16),
            pltpu.VMEM((frames,) + slab, bf16),
            pltpu.VMEM((frames,) + flat, f32),
            pltpu.VMEM((frames,) + flat, bf16),
            pltpu.VMEM(flat, f32),
            pltpu.VMEM(flat, f32),
            pltpu.VMEM((3,) + slab, bf16),
            pltpu.VMEM(slab, bf16),
            pltpu.VMEM(slab, bf16),
            pltpu.VMEM(args[6].shape, f32),
            pltpu.VMEM(args[7].shape, f32),
            dma((chunks,)), dma((6,)), dma((rows, chunks)),
            dma((chips, chunks)), dma((chips, chunks)), dma((chips, chunks)),
            dma((frames,)), dma((frames,)), dma((frames, chunks)), dma((frames, chunks)),
            dma((2, chunks)), dma((2, chunks)), dma((2,)),
        ],
        compiler_params=pltpu.CompilerParams(collective_id=0, has_side_effects=True),
        name="block",
    )(*args)


def solution(mesh):
    split = P("frame", "row", None, None)
    return jax.shard_map(
        functools.partial(on_device, mesh.shape["frame"], mesh.shape["row"]),
        mesh=mesh,
        in_specs=(split,) * 6 + (P(), P()),
        out_specs=(split, split),
        check_vma=False,
    )
```

```python
import functools
import math

import jax
import jax.numpy as jnp
from jax import lax
from jax.experimental import pallas as pl
from jax.experimental.pallas import tpu as pltpu
from jax.sharding import PartitionSpec as P

HEAD_DIM = 64
LANES = 2 * HEAD_DIM
SCALE = HEAD_DIM ** (-0.5)
LOG2E = math.log2(math.e)


def block_kernel(
    frames, rows, chunks, tokens, lent,
    res_hbm, q_hbm, k_hbm, v_hbm, qt_hbm, kt_hbm, cw_hbm, cb_hbm,
    so_hbm, bo_hbm,
    kv, qs, qh, oh, rs, qts, ktb, hb, tsc, wts, peak, rden, mixb, sob, bob, cwv, cbv,
    ld_kv, ld_misc, kv_recv, up_send, dn_send, pt_send,
    kt_recv, kt_send, h_recv, h_send, halo_recv, halo_send, out_sem, lend_sem, give_sem, back_sem,
):
    me_f = lax.axis_index("frame")
    me_r = lax.axis_index("row")
    chips = rows // 2
    z = me_r // 2
    core = me_r % 2
    at_end = jnp.logical_or(z == 0, z == chips - 1)
    helps = jnp.logical_or(z == 1, z == chips - 2)
    mate = me_r + 2 * jnp.where(jnp.logical_or(z == 0, z == chips - 2), 1, -1)

    def has_up(c):
        return z < chips - 1 - (1 if c < lent else 0)

    def has_down(c):
        return z > (1 if c < lent else 0)

    def attends(c):
        return jnp.logical_not(at_end) if c < lent else z >= 0

    def lanes(c):
        return pl.ds(c * LANES, LANES)

    for c in range(chunks):
        pltpu.make_async_copy(k_hbm.at[0, 0, :, lanes(c)], kv.at[me_r, c, 0], ld_kv.at[c]).start()
        pltpu.make_async_copy(v_hbm.at[0, 0, :, lanes(c)], kv.at[me_r, c, 1], ld_kv.at[c]).start()
    for c in range(chunks):
        pltpu.make_async_copy(kt_hbm.at[0, 0, :, lanes(c)], ktb.at[me_f, c], ld_misc.at[0]).start()
    for c in range(chunks):
        pltpu.make_async_copy(qt_hbm.at[0, 0, :, lanes(c)], qts.at[c], ld_misc.at[1]).start()
        pltpu.make_async_copy(q_hbm.at[0, 0, :, lanes(c)], qs.at[c], ld_misc.at[2]).start()
        pltpu.make_async_copy(res_hbm.at[0, 0, :, lanes(c)], rs.at[c], ld_misc.at[3]).start()
    pltpu.make_async_copy(cw_hbm, cwv, ld_misc.at[4]).start()
    pltpu.make_async_copy(cb_hbm, cbv, ld_misc.at[5]).start()

    barrier = pltpu.get_barrier_semaphore()

    def greet(**where):
        pl.semaphore_signal(
            barrier, inc=1, device_id=where, device_id_type=pl.DeviceIdType.MESH
        )

    greet(row=me_r + 1 - 2 * core)

    @pl.when(z > 0)
    def _():
        greet(row=me_r - 2)

    @pl.when(z < chips - 1)
    def _():
        greet(row=me_r + 2)

    across = me_r - 1 + 2 * core
    has_across = jnp.logical_and(across >= 0, across < rows)

    @pl.when(has_across)
    def _():
        greet(row=across)

    @pl.loop(1, frames)
    def _(step):
        greet(frame=(me_f + step) % frames)

    pl.semaphore_wait(
        barrier,
        frames
        + (z > 0).astype(jnp.int32)
        + (z < chips - 1).astype(jnp.int32)
        + has_across.astype(jnp.int32),
    )

    def remote(src, dst, send, recv, **where):
        return pltpu.make_async_remote_copy(
            src_ref=src, dst_ref=dst, send_sem=send, recv_sem=recv,
            device_id=where, device_id_type=pl.DeviceIdType.MESH,
        )

    def kv_copy(chip, of_core, c, send, to_row):
        src = 2 * chip + of_core
        return remote(kv.at[src, c], kv.at[src, c], send, kv_recv.at[src, c], row=to_row)

    def go_up(chip, c):
        return kv_copy(chip, core, c, up_send.at[chip, c], me_r + 2)

    def go_down(chip, c):
        return kv_copy(chip, core, c, dn_send.at[chip, c], me_r - 2)

    def to_partner(chip, c):
        return kv_copy(chip, core, c, pt_send.at[chip, c], me_r + 1 - 2 * core)

    def wait_slot(chip, of_core, c):
        kv_copy(chip, of_core, c, up_send.at[chip, c], me_r + 1 - 2 * core).wait_recv()

    def kt_copy(g, to):
        return remote(ktb.at[g], ktb.at[g], kt_send.at[to], kt_recv.at[g], frame=to)

    def h_copy(g, to, c):
        return remote(hb.at[g, c], hb.at[g, c], h_send.at[to, c], h_recv.at[g, c], frame=to)

    def halo_copy(side, c):
        return remote(
            mixb.at[1, c], mixb.at[2 - 2 * side, c], halo_send.at[side, c],
            halo_recv.at[1 - side, c], row=me_r - 1 + 2 * side,
        )

    def lend():
        return remote(qs.at[pl.ds(0, lent)], qh, lend_sem.at[0], lend_sem.at[1], row=mate)

    def give_back(c):
        return remote(oh.at[c], sob.at[c], give_sem.at[c], back_sem.at[c], row=mate)

    for c in range(chunks):
        pltpu.make_async_copy(kv.at[me_r, c], kv.at[me_r, c], ld_kv.at[c]).wait()

        @pl.when(has_down(c))
        def _(c=c):
            go_down(z, c).start()

        @pl.when(has_up(c))
        def _(c=c):
            go_up(z, c).start()

        @pl.when(attends(c))
        def _(c=c):
            to_partner(z, c).start()

    pltpu.make_async_copy(qs, qs, ld_misc.at[2]).wait()
    if lent:
        @pl.when(at_end)
        def _():
            lend().start()

    pltpu.make_async_copy(ktb.at[me_f], ktb.at[me_f], ld_misc.at[0]).wait()

    @pl.loop(me_f + 1, frames)
    def _(to):
        kt_copy(me_f, to).start()

    def relay(d, c):
        @pl.when(jnp.logical_and(z - d >= 0, attends(c)))
        def _():
            wait_slot(z - d, core, c)

            @pl.when(has_up(c))
            def _():
                go_up(z - d, c).start()

            to_partner(z - d, c).start()

        @pl.when(jnp.logical_and(z + d < chips, attends(c)))
        def _():
            wait_slot(z + d, core, c)

            @pl.when(has_down(c))
            def _():
                go_down(z + d, c).start()

            to_partner(z + d, c).start()

    @pl.loop(1, chips - 1)
    def _(d):
        for c in range(chunks):
            relay(d, c)

    pltpu.make_async_copy(qts, qts, ld_misc.at[1]).wait()

    @pl.loop(0, me_f)
    def _(g):
        kt_copy(g, me_f).wait_recv()

    flat = chunks * tokens
    same = (
        (lax.broadcasted_iota(jnp.int32, (2 * LANES, LANES), 0) // HEAD_DIM) % 2
        == lax.broadcasted_iota(jnp.int32, (2 * LANES, LANES), 1) // HEAD_DIM
    )
    spread = jnp.where(same, 1.0, 0.0).astype(jnp.bfloat16)
    peak[...] = jnp.full(peak.shape, -1e30, jnp.float32)

    @pl.loop(0, me_f + 1)
    def _(g):
        product = (
            qts[...].reshape(flat, LANES).astype(jnp.float32)
            * ktb[g].reshape(flat, LANES).astype(jnp.float32)
        )
        high = product.astype(jnp.bfloat16)
        low = (product - high.astype(jnp.float32)).astype(jnp.bfloat16)
        score = jnp.dot(
            jnp.concatenate([high, low], axis=1), spread, preferred_element_type=jnp.float32
        )
        tsc[g] = score
        peak[...] = jnp.maximum(peak[...], score)

    rden[...] = jnp.zeros(rden.shape, jnp.float32)

    @pl.loop(0, me_f + 1)
    def _(g):
        raised = jnp.exp2((tsc[g] - peak[...]) * (SCALE * LOG2E))
        rden[...] += raised
        wts[g] = raised.astype(jnp.bfloat16)

    rden[...] = 1.0 / rden[...]

    pltpu.make_async_copy(rs, rs, ld_misc.at[3]).wait()

    first_head = lax.broadcasted_iota(jnp.int32, (tokens, LANES), 1) < HEAD_DIM
    keys = rows * tokens

    def attend(blocks, c):
        none = jnp.zeros_like(blocks[0])
        queries = jnp.concatenate(
            [part for q in blocks
             for part in (jnp.where(first_head, q, none), jnp.where(first_head, none, q))],
            axis=0,
        )
        scores = lax.dot_general(
            queries, kv[:, c, 0].reshape(keys, LANES), (((1,), (1,)), ((), ())),
            preferred_element_type=jnp.float32,
        )
        top = jnp.max(scores, axis=1, keepdims=True)
        raised = jnp.exp2((scores - top) * (SCALE * LOG2E))
        denom = jnp.sum(raised, axis=1, keepdims=True)
        both = jnp.dot(
            raised.astype(jnp.bfloat16), kv[:, c, 1].reshape(keys, LANES),
            preferred_element_type=jnp.float32,
        ) / denom
        return [
            jnp.where(
                first_head,
                both[2 * i * tokens : (2 * i + 1) * tokens],
                both[(2 * i + 1) * tokens : (2 * i + 2) * tokens],
            ).astype(jnp.bfloat16)
            for i in range(len(blocks))
        ]

    for c in range(chunks):
        relay(chips - 1, c)

        @pl.when(attends(c))
        def _(c=c):
            @pl.loop(0, chips)
            def _(chip):
                wait_slot(chip, 1 - core, c)

        if c < lent:
            @pl.when(helps)
            def _(c=c):
                if c == 0:
                    lend().wait_recv()
                sob[c], oh[c] = attend([qs[c], qh[c]], c)
                give_back(c).start()

            @pl.when(at_end)
            def _(c=c):
                give_back(c).wait_recv()

            if chips > 4:
                @pl.when(jnp.logical_not(jnp.logical_or(at_end, helps)))
                def _(c=c):
                    sob[c] = attend([qs[c]], c)[0]
        else:
            sob[c] = attend([qs[c]], c)[0]

        hb[me_f, c] = (rs[c].astype(jnp.float32) + sob[c].astype(jnp.float32)).astype(jnp.bfloat16)

        @pl.loop(me_f + 1, frames)
        def _(to, c=c):
            h_copy(me_f, to, c).start()

        pltpu.make_async_copy(sob.at[c], so_hbm.at[0, 0, :, lanes(c)], out_sem.at[0]).start()

    for c in range(chunks):
        @pl.loop(0, me_f)
        def _(g, c=c):
            h_copy(g, me_f, c).wait_recv()

        here = pl.ds(c * tokens, tokens)

        def add(g, total):
            return total + wts[g, here].astype(jnp.float32) * hb[g, c].astype(jnp.float32)

        total = lax.fori_loop(0, me_f + 1, add, jnp.zeros((tokens, LANES), jnp.float32))
        temporal = (total * rden[here]).astype(jnp.bfloat16)
        mixb[1, c] = (
            hb[me_f, c].astype(jnp.float32) + temporal.astype(jnp.float32)
        ).astype(jnp.bfloat16)

        @pl.when(me_r > 0)
        def _(c=c):
            halo_copy(0, c).start()

        @pl.when(me_r < rows - 1)
        def _(c=c):
            halo_copy(1, c).start()

    pltpu.make_async_copy(cwv, cwv, ld_misc.at[4]).wait()
    pltpu.make_async_copy(cbv, cbv, ld_misc.at[5]).wait()

    @pl.when(me_r == 0)
    def _():
        mixb[0] = jnp.zeros(mixb.shape[1:], mixb.dtype)

    @pl.when(me_r == rows - 1)
    def _():
        mixb[2] = jnp.zeros(mixb.shape[1:], mixb.dtype)

    position = lax.broadcasted_iota(jnp.int32, (tokens, LANES), 0)
    for c in range(chunks):
        @pl.when(me_r > 0)
        def _(c=c):
            remote(
                mixb.at[0, c], mixb.at[0, c], halo_send.at[0, c], halo_recv.at[0, c],
                row=me_r - 1,
            ).wait_recv()

        @pl.when(me_r < rows - 1)
        def _(c=c):
            remote(
                mixb.at[2, c], mixb.at[2, c], halo_send.at[1, c], halo_recv.at[1, c],
                row=me_r + 1,
            ).wait_recv()

        lines = [mixb[a, c].astype(jnp.float32) for a in range(3)]
        taps = [
            sum(cwv[a, pl.ds(b, 1), lanes(c)] * lines[a] for a in range(3)) for b in range(3)
        ]
        left = jnp.where(position == 0, 0.0, pltpu.roll(taps[0], 1, 0))
        right = jnp.where(position == tokens - 1, 0.0, pltpu.roll(taps[2], tokens - 1, 0))
        conv = cbv[pl.ds(c * LANES, LANES)].reshape(1, LANES) + taps[1] + left + right
        inner = math.sqrt(2.0 / math.pi) * (conv + 0.044715 * (conv * conv * conv))
        bob[c] = (lines[1] + 0.5 * conv * (1.0 + jnp.tanh(inner))).astype(jnp.bfloat16)
        pltpu.make_async_copy(bob.at[c], bo_hbm.at[0, 0, :, lanes(c)], out_sem.at[1]).start()

    @pl.loop(0, chips)
    def _(chip):
        for c in range(chunks):
            @pl.when(attends(c))
            def _(c=c):
                to_partner(chip, c).wait_send()

            @pl.when(jnp.logical_and(jnp.logical_and(chip <= z, has_up(c)), jnp.logical_or(attends(c), chip == z)))
            def _(c=c):
                go_up(chip, c).wait_send()

            @pl.when(jnp.logical_and(jnp.logical_and(chip >= z, has_down(c)), jnp.logical_or(attends(c), chip == z)))
            def _(c=c):
                go_down(chip, c).wait_send()

    @pl.loop(me_f + 1, frames)
    def _(to):
        kt_copy(me_f, to).wait_send()
        for c in range(chunks):
            h_copy(me_f, to, c).wait_send()

    for c in range(chunks):
        @pl.when(me_r > 0)
        def _(c=c):
            halo_copy(0, c).wait_send()

        @pl.when(me_r < rows - 1)
        def _(c=c):
            halo_copy(1, c).wait_send()

    if lent:
        @pl.when(at_end)
        def _():
            lend().wait_send()

    for c in range(lent):
        @pl.when(helps)
        def _(c=c):
            give_back(c).wait_send()

    pltpu.make_async_copy(sob, sob, out_sem.at[0]).wait()
    pltpu.make_async_copy(bob, bob, out_sem.at[1]).wait()


def on_device(frames, rows, *args):
    block = args[0]
    _, _, tokens, channels = block.shape
    chunks = channels // LANES
    chips = rows // 2
    lent = chunks // 2 if chips >= 4 else 0
    held = max(lent, 1)
    slab = (chunks, tokens, LANES)
    flat = (chunks * tokens, LANES)
    bf16, f32 = jnp.bfloat16, jnp.float32
    dma = pltpu.SemaphoreType.DMA
    anywhere = pl.BlockSpec(memory_space=pl.ANY)
    return pl.pallas_call(
        functools.partial(block_kernel, frames, rows, chunks, tokens, lent),
        out_shape=(jax.ShapeDtypeStruct(block.shape, bf16),) * 2,
        in_specs=[anywhere] * 8,
        out_specs=(anywhere, anywhere),
        scratch_shapes=[
            pltpu.VMEM((rows, chunks, 2, tokens, LANES), bf16),
            pltpu.VMEM(slab, bf16),
            pltpu.VMEM((held,) + slab[1:], bf16),
            pltpu.VMEM((held,) + slab[1:], bf16),
            pltpu.VMEM(slab, bf16),
            pltpu.VMEM(slab, bf16),
            pltpu.VMEM((frames,) + slab, bf16),
            pltpu.VMEM((frames,) + slab, bf16),
            pltpu.VMEM((frames,) + flat, f32),
            pltpu.VMEM((frames,) + flat, bf16),
            pltpu.VMEM(flat, f32),
            pltpu.VMEM(flat, f32),
            pltpu.VMEM((3,) + slab, bf16),
            pltpu.VMEM(slab, bf16),
            pltpu.VMEM(slab, bf16),
            pltpu.VMEM(args[6].shape, f32),
            pltpu.VMEM(args[7].shape, f32),
            dma((chunks,)), dma((6,)), dma((rows, chunks)),
            dma((chips, chunks)), dma((chips, chunks)), dma((chips, chunks)),
            dma((frames,)), dma((frames,)), dma((frames, chunks)), dma((frames, chunks)),
            dma((2, chunks)), dma((2, chunks)), dma((2,)),
            dma((2,)), dma((held,)), dma((held,)),
        ],
        compiler_params=pltpu.CompilerParams(collective_id=0, has_side_effects=True),
        name="block",
    )(*args)


def solution(mesh):
    split = P("frame", "row", None, None)
    return jax.shard_map(
        functools.partial(on_device, mesh.shape["frame"], mesh.shape["row"]),
        mesh=mesh,
        in_specs=(split,) * 6 + (P(), P()),
        out_specs=(split, split),
        check_vma=False,
    )
```

```python
import functools
import math

import jax
import jax.numpy as jnp
from jax import lax
from jax.experimental import pallas as pl
from jax.experimental.pallas import tpu as pltpu
from jax.sharding import PartitionSpec as P

HEAD_DIM = 64
LANES = 2 * HEAD_DIM
SCALE = HEAD_DIM ** (-0.5)
LOG2E = math.log2(math.e)


def block_kernel(
    frames, rows, chunks, tokens, lent,
    res_hbm, q_hbm, k_hbm, v_hbm, qt_hbm, kt_hbm, cw_hbm, cb_hbm,
    so_hbm, bo_hbm,
    kv, qs, qh, oh, rs, qts, ktb, hb, tsc, wts, peak, rden, mixb, sob, bob, cwv, cbv,
    ld_kv, ld_misc, kv_recv, up_send, dn_send, pt_send,
    kt_recv, kt_send, h_recv, h_send, halo_recv, halo_send, out_sem, lend_sem, give_sem, back_sem,
):
    me_f = lax.axis_index("frame")
    me_r = lax.axis_index("row")
    chips = rows // 2
    z = me_r // 2
    core = me_r % 2
    at_end = jnp.logical_or(z == 0, z == chips - 1)
    helps = jnp.logical_or(z == 1, z == chips - 2)
    mate = me_r + 2 * jnp.where(jnp.logical_or(z == 0, z == chips - 2), 1, -1)

    def has_up(c):
        return z < chips - 1 - (1 if c < lent else 0)

    def has_down(c):
        return z > (1 if c < lent else 0)

    def attends(c):
        return jnp.logical_not(at_end) if c < lent else z >= 0

    def lanes(c):
        return pl.ds(c * LANES, LANES)

    for c in range(chunks):
        pltpu.make_async_copy(k_hbm.at[0, 0, :, lanes(c)], kv.at[me_r, c, 0], ld_kv.at[c]).start()
        pltpu.make_async_copy(v_hbm.at[0, 0, :, lanes(c)], kv.at[me_r, c, 1], ld_kv.at[c]).start()
    for c in range(chunks):
        pltpu.make_async_copy(kt_hbm.at[0, 0, :, lanes(c)], ktb.at[me_f, c], ld_misc.at[0]).start()
    for c in range(chunks):
        pltpu.make_async_copy(qt_hbm.at[0, 0, :, lanes(c)], qts.at[c], ld_misc.at[1]).start()
        pltpu.make_async_copy(q_hbm.at[0, 0, :, lanes(c)], qs.at[c], ld_misc.at[2]).start()
        pltpu.make_async_copy(res_hbm.at[0, 0, :, lanes(c)], rs.at[c], ld_misc.at[3]).start()
    pltpu.make_async_copy(cw_hbm, cwv, ld_misc.at[4]).start()
    pltpu.make_async_copy(cb_hbm, cbv, ld_misc.at[5]).start()

    barrier = pltpu.get_barrier_semaphore()

    def greet(**where):
        pl.semaphore_signal(
            barrier, inc=1, device_id=where, device_id_type=pl.DeviceIdType.MESH
        )

    greet(row=me_r + 1 - 2 * core)

    @pl.when(z > 0)
    def _():
        greet(row=me_r - 2)

    @pl.when(z < chips - 1)
    def _():
        greet(row=me_r + 2)

    across = me_r - 1 + 2 * core
    has_across = jnp.logical_and(across >= 0, across < rows)

    @pl.when(has_across)
    def _():
        greet(row=across)

    @pl.loop(1, frames)
    def _(step):
        greet(frame=(me_f + step) % frames)

    pl.semaphore_wait(
        barrier,
        frames
        + (z > 0).astype(jnp.int32)
        + (z < chips - 1).astype(jnp.int32)
        + has_across.astype(jnp.int32),
    )

    def remote(src, dst, send, recv, **where):
        return pltpu.make_async_remote_copy(
            src_ref=src, dst_ref=dst, send_sem=send, recv_sem=recv,
            device_id=where, device_id_type=pl.DeviceIdType.MESH,
        )

    def kv_copy(chip, of_core, c, send, to_row):
        src = 2 * chip + of_core
        return remote(kv.at[src, c], kv.at[src, c], send, kv_recv.at[src, c], row=to_row)

    def go_up(chip, c):
        return kv_copy(chip, core, c, up_send.at[chip], me_r + 2)

    def go_down(chip, c):
        return kv_copy(chip, core, c, dn_send.at[chip], me_r - 2)

    def to_partner(chip, c):
        return kv_copy(chip, core, c, pt_send.at[chip], me_r + 1 - 2 * core)

    def wait_slot(chip, of_core, c):
        kv_copy(chip, of_core, c, up_send.at[chip], me_r + 1 - 2 * core).wait_recv()

    def kt_copy(g, to):
        return remote(ktb.at[g], ktb.at[g], kt_send.at[to], kt_recv.at[g], frame=to)

    def h_copy(g, to, c):
        return remote(hb.at[g, c], hb.at[g, c], h_send.at[to], h_recv.at[g, c], frame=to)

    def halo_copy(side, c):
        return remote(
            mixb.at[1, c], mixb.at[2 - 2 * side, c], halo_send.at[side],
            halo_recv.at[1 - side, c], row=me_r - 1 + 2 * side,
        )

    def lend():
        return remote(qs.at[pl.ds(0, lent)], qh, lend_sem.at[0], lend_sem.at[1], row=mate)

    def give_back(c):
        return remote(oh.at[c], sob.at[c], give_sem.at[c], back_sem.at[c], row=mate)

    for c in range(chunks):
        pltpu.make_async_copy(kv.at[me_r, c], kv.at[me_r, c], ld_kv.at[c]).wait()

        @pl.when(has_down(c))
        def _(c=c):
            go_down(z, c).start()

        @pl.when(has_up(c))
        def _(c=c):
            go_up(z, c).start()

        @pl.when(attends(c))
        def _(c=c):
            to_partner(z, c).start()

    pltpu.make_async_copy(qs, qs, ld_misc.at[2]).wait()
    if lent:
        @pl.when(at_end)
        def _():
            lend().start()

    pltpu.make_async_copy(ktb.at[me_f], ktb.at[me_f], ld_misc.at[0]).wait()

    @pl.loop(me_f + 1, frames)
    def _(to):
        kt_copy(me_f, to).start()

    def relay(d, c):
        @pl.when(jnp.logical_and(z - d >= 0, attends(c)))
        def _():
            wait_slot(z - d, core, c)

            @pl.when(has_up(c))
            def _():
                go_up(z - d, c).start()

            to_partner(z - d, c).start()

        @pl.when(jnp.logical_and(z + d < chips, attends(c)))
        def _():
            wait_slot(z + d, core, c)

            @pl.when(has_down(c))
            def _():
                go_down(z + d, c).start()

            to_partner(z + d, c).start()

    last = jnp.maximum(z, chips - 1 - z)

    @pl.loop(1, last)
    def _(d):
        for c in range(chunks):
            relay(d, c)

    pltpu.make_async_copy(rs, rs, ld_misc.at[3]).wait()

    first_head = lax.broadcasted_iota(jnp.int32, (tokens, LANES), 1) < HEAD_DIM
    keys = rows * tokens

    def attend(blocks, c):
        none = jnp.zeros_like(blocks[0])
        queries = jnp.concatenate(
            [part for q in blocks
             for part in (jnp.where(first_head, q, none), jnp.where(first_head, none, q))],
            axis=0,
        )
        scores = lax.dot_general(
            queries, kv[:, c, 0].reshape(keys, LANES), (((1,), (1,)), ((), ())),
            preferred_element_type=jnp.float32,
        )
        top = jnp.max(scores, axis=1, keepdims=True)
        raised = jnp.exp2((scores - top) * (SCALE * LOG2E))
        denom = jnp.sum(raised, axis=1, keepdims=True)
        both = jnp.dot(
            raised.astype(jnp.bfloat16), kv[:, c, 1].reshape(keys, LANES),
            preferred_element_type=jnp.float32,
        ) / denom
        return [
            jnp.where(
                first_head,
                both[2 * i * tokens : (2 * i + 1) * tokens],
                both[(2 * i + 1) * tokens : (2 * i + 2) * tokens],
            ).astype(jnp.bfloat16)
            for i in range(len(blocks))
        ]

    for c in range(chunks):
        relay(last, c)

        @pl.when(attends(c))
        def _(c=c):
            @pl.loop(0, chips)
            def _(chip):
                wait_slot(chip, 1 - core, c)

        if c < lent:
            @pl.when(helps)
            def _(c=c):
                if c == 0:
                    lend().wait_recv()
                sob[c], oh[c] = attend([qs[c], qh[c]], c)
                give_back(c).start()

            @pl.when(at_end)
            def _(c=c):
                give_back(c).wait_recv()

            if chips > 4:
                @pl.when(jnp.logical_not(jnp.logical_or(at_end, helps)))
                def _(c=c):
                    sob[c] = attend([qs[c]], c)[0]
        else:
            sob[c] = attend([qs[c]], c)[0]

        hb[me_f, c] = (rs[c].astype(jnp.float32) + sob[c].astype(jnp.float32)).astype(jnp.bfloat16)

        @pl.loop(me_f + 1, frames)
        def _(to, c=c):
            h_copy(me_f, to, c).start()

        pltpu.make_async_copy(sob.at[c], so_hbm.at[0, 0, :, lanes(c)], out_sem.at[0]).start()

    pltpu.make_async_copy(qts, qts, ld_misc.at[1]).wait()

    @pl.loop(0, me_f)
    def _(g):
        kt_copy(g, me_f).wait_recv()

    flat = chunks * tokens
    same = (
        (lax.broadcasted_iota(jnp.int32, (2 * LANES, LANES), 0) // HEAD_DIM) % 2
        == lax.broadcasted_iota(jnp.int32, (2 * LANES, LANES), 1) // HEAD_DIM
    )
    spread = jnp.where(same, 1.0, 0.0).astype(jnp.bfloat16)
    peak[...] = jnp.full(peak.shape, -1e30, jnp.float32)

    @pl.loop(0, me_f + 1)
    def _(g):
        product = (
            qts[...].reshape(flat, LANES).astype(jnp.float32)
            * ktb[g].reshape(flat, LANES).astype(jnp.float32)
        )
        high = product.astype(jnp.bfloat16)
        low = (product - high.astype(jnp.float32)).astype(jnp.bfloat16)
        score = jnp.dot(
            jnp.concatenate([high, low], axis=1), spread, preferred_element_type=jnp.float32
        )
        tsc[g] = score
        peak[...] = jnp.maximum(peak[...], score)

    rden[...] = jnp.zeros(rden.shape, jnp.float32)

    @pl.loop(0, me_f + 1)
    def _(g):
        raised = jnp.exp2((tsc[g] - peak[...]) * (SCALE * LOG2E))
        rden[...] += raised
        wts[g] = raised.astype(jnp.bfloat16)

    rden[...] = 1.0 / rden[...]

    for c in range(chunks):
        @pl.loop(0, me_f)
        def _(g, c=c):
            h_copy(g, me_f, c).wait_recv()

        here = pl.ds(c * tokens, tokens)

        def add(g, total):
            return total + wts[g, here].astype(jnp.float32) * hb[g, c].astype(jnp.float32)

        total = lax.fori_loop(0, me_f + 1, add, jnp.zeros((tokens, LANES), jnp.float32))
        temporal = (total * rden[here]).astype(jnp.bfloat16)
        mixb[1, c] = (
            hb[me_f, c].astype(jnp.float32) + temporal.astype(jnp.float32)
        ).astype(jnp.bfloat16)

        @pl.when(me_r > 0)
        def _(c=c):
            halo_copy(0, c).start()

        @pl.when(me_r < rows - 1)
        def _(c=c):
            halo_copy(1, c).start()

    pltpu.make_async_copy(cwv, cwv, ld_misc.at[4]).wait()
    pltpu.make_async_copy(cbv, cbv, ld_misc.at[5]).wait()

    @pl.when(me_r == 0)
    def _():
        mixb[0] = jnp.zeros(mixb.shape[1:], mixb.dtype)

    @pl.when(me_r == rows - 1)
    def _():
        mixb[2] = jnp.zeros(mixb.shape[1:], mixb.dtype)

    position = lax.broadcasted_iota(jnp.int32, (tokens, LANES), 0)
    for c in range(chunks):
        @pl.when(me_r > 0)
        def _(c=c):
            remote(
                mixb.at[0, c], mixb.at[0, c], halo_send.at[0], halo_recv.at[0, c],
                row=me_r - 1,
            ).wait_recv()

        @pl.when(me_r < rows - 1)
        def _(c=c):
            remote(
                mixb.at[2, c], mixb.at[2, c], halo_send.at[1], halo_recv.at[1, c],
                row=me_r + 1,
            ).wait_recv()

        lines = [mixb[a, c].astype(jnp.float32) for a in range(3)]
        taps = [
            sum(cwv[a, pl.ds(b, 1), lanes(c)] * lines[a] for a in range(3)) for b in range(3)
        ]
        left = jnp.where(position == 0, 0.0, pltpu.roll(taps[0], 1, 0))
        right = jnp.where(position == tokens - 1, 0.0, pltpu.roll(taps[2], tokens - 1, 0))
        conv = cbv[pl.ds(c * LANES, LANES)].reshape(1, LANES) + taps[1] + left + right
        inner = math.sqrt(2.0 / math.pi) * (conv + 0.044715 * (conv * conv * conv))
        bob[c] = (lines[1] + 0.5 * conv * (1.0 + jnp.tanh(inner))).astype(jnp.bfloat16)
        pltpu.make_async_copy(bob.at[c], bo_hbm.at[0, 0, :, lanes(c)], out_sem.at[1]).start()

    def drain(ref, sem):
        pltpu.make_async_copy(ref, ref, sem).wait()

    some = pl.ds(lent, chunks - lent)

    @pl.loop(0, chips)
    def _(chip):
        src = 2 * chip + core

        @pl.when(at_end)
        def _():
            drain(kv.at[src, some], pt_send.at[chip])

        @pl.when(jnp.logical_not(at_end))
        def _():
            drain(kv.at[src], pt_send.at[chip])

    bound = 1 if lent else 0

    @pl.loop(0, z + 1)
    def _(chip):
        @pl.when(z < chips - 1 - bound)
        def _():
            drain(kv.at[2 * chip + core], up_send.at[chip])

        @pl.when(jnp.logical_and(z < chips - 1, z >= chips - 1 - bound))
        def _():
            drain(kv.at[2 * chip + core, some], up_send.at[chip])

    @pl.loop(z, chips)
    def _(chip):
        @pl.when(z > bound)
        def _():
            drain(kv.at[2 * chip + core], dn_send.at[chip])

        @pl.when(jnp.logical_and(z > 0, z <= bound))
        def _():
            drain(kv.at[2 * chip + core, some], dn_send.at[chip])

    @pl.loop(me_f + 1, frames)
    def _(to):
        kt_copy(me_f, to).wait_send()
        drain(hb.at[me_f], h_send.at[to])

    @pl.when(me_r > 0)
    def _():
        drain(mixb.at[1], halo_send.at[0])

    @pl.when(me_r < rows - 1)
    def _():
        drain(mixb.at[1], halo_send.at[1])

    if lent:
        @pl.when(at_end)
        def _():
            lend().wait_send()

    for c in range(lent):
        @pl.when(helps)
        def _(c=c):
            give_back(c).wait_send()

    pltpu.make_async_copy(sob, sob, out_sem.at[0]).wait()
    pltpu.make_async_copy(bob, bob, out_sem.at[1]).wait()


def on_device(frames, rows, *args):
    block = args[0]
    _, _, tokens, channels = block.shape
    chunks = channels // LANES
    chips = rows // 2
    lent = chunks * 3 // 6 if chips >= 4 else 0
    held = max(lent, 1)
    slab = (chunks, tokens, LANES)
    flat = (chunks * tokens, LANES)
    bf16, f32 = jnp.bfloat16, jnp.float32
    dma = pltpu.SemaphoreType.DMA
    anywhere = pl.BlockSpec(memory_space=pl.ANY)
    return pl.pallas_call(
        functools.partial(block_kernel, frames, rows, chunks, tokens, lent),
        out_shape=(jax.ShapeDtypeStruct(block.shape, bf16),) * 2,
        in_specs=[anywhere] * 8,
        out_specs=(anywhere, anywhere),
        scratch_shapes=[
            pltpu.VMEM((rows, chunks, 2, tokens, LANES), bf16),
            pltpu.VMEM(slab, bf16),
            pltpu.VMEM((held,) + slab[1:], bf16),
            pltpu.VMEM((held,) + slab[1:], bf16),
            pltpu.VMEM(slab, bf16),
            pltpu.VMEM(slab, bf16),
            pltpu.VMEM((frames,) + slab, bf16),
            pltpu.VMEM((frames,) + slab, bf16),
            pltpu.VMEM((frames,) + flat, f32),
            pltpu.VMEM((frames,) + flat, bf16),
            pltpu.VMEM(flat, f32),
            pltpu.VMEM(flat, f32),
            pltpu.VMEM((3,) + slab, bf16),
            pltpu.VMEM(slab, bf16),
            pltpu.VMEM(slab, bf16),
            pltpu.VMEM(args[6].shape, f32),
            pltpu.VMEM(args[7].shape, f32),
            dma((chunks,)), dma((6,)), dma((rows, chunks)),
            dma((chips,)), dma((chips,)), dma((chips,)),
            dma((frames,)), dma((frames,)), dma((frames, chunks)), dma((frames,)),
            dma((2, chunks)), dma((2,)), dma((2,)),
            dma((2,)), dma((held,)), dma((held,)),
        ],
        compiler_params=pltpu.CompilerParams(collective_id=0, has_side_effects=True,
            vmem_limit_bytes=(14 << 20) + (rows << 18) + (frames << 19)),
        name="block",
    )(*[pltpu.with_memory_space_constraint(a, pltpu.HBM) for a in args])


def solution(mesh):
    split = P("frame", "row", None, None)
    return jax.shard_map(
        functools.partial(on_device, mesh.shape["frame"], mesh.shape["row"]),
        mesh=mesh,
        in_specs=(split,) * 6 + (P(), P()),
        out_specs=(split, split),
        check_vma=False,
    )
```

```python
import functools
import math

import jax
import jax.numpy as jnp
from jax import lax
from jax.experimental import pallas as pl
from jax.experimental.pallas import tpu as pltpu
from jax.sharding import PartitionSpec as P

HEAD_DIM = 64
LANES = 2 * HEAD_DIM
SCALE = HEAD_DIM ** (-0.5)
LOG2E = math.log2(math.e)


def block_kernel(
    frames, rows, chunks, tokens, lent,
    res_hbm, q_hbm, k_hbm, v_hbm, qt_hbm, kt_hbm, cw_hbm, cb_hbm,
    so_hbm, bo_hbm,
    kv, qs, qh, oh, rs, qts, ktb, hb, tsc, wts, peak, rden, mixb, sob, bob, cwv, cbv,
    ld_kv, ld_misc, kv_recv, up_send, dn_send, pt_send,
    kt_recv, kt_send, h_recv, h_send, halo_recv, halo_send, out_sem, lend_sem, give_sem, back_sem,
):
    me_f = lax.axis_index("frame")
    me_r = lax.axis_index("row")
    chips = rows // 2
    z = me_r // 2
    core = me_r % 2
    at_end = jnp.logical_or(z == 0, z == chips - 1)
    helps = jnp.logical_or(z == 1, z == chips - 2)
    mate = me_r + 2 * jnp.where(jnp.logical_or(z == 0, z == chips - 2), 1, -1)

    def has_up(c):
        return z < chips - 1 - (1 if c < lent else 0)

    def has_down(c):
        return z > (1 if c < lent else 0)

    def attends(c):
        return jnp.logical_not(at_end) if c < lent else z >= 0

    def lanes(c):
        return pl.ds(c * LANES, LANES)

    for c in range(chunks):
        pltpu.make_async_copy(k_hbm.at[0, 0, :, lanes(c)], kv.at[me_r, c, 0], ld_kv.at[c]).start()
        pltpu.make_async_copy(v_hbm.at[0, 0, :, lanes(c)], kv.at[me_r, c, 1], ld_kv.at[c]).start()
    for c in range(chunks):
        pltpu.make_async_copy(kt_hbm.at[0, 0, :, lanes(c)], ktb.at[me_f, c], ld_misc.at[0]).start()
    for c in range(chunks):
        pltpu.make_async_copy(qt_hbm.at[0, 0, :, lanes(c)], qts.at[c], ld_misc.at[1]).start()
        pltpu.make_async_copy(q_hbm.at[0, 0, :, lanes(c)], qs.at[c], ld_misc.at[2]).start()
        pltpu.make_async_copy(res_hbm.at[0, 0, :, lanes(c)], rs.at[c], ld_misc.at[3]).start()
    pltpu.make_async_copy(cw_hbm, cwv, ld_misc.at[4]).start()
    pltpu.make_async_copy(cb_hbm, cbv, ld_misc.at[5]).start()

    barrier = pltpu.get_barrier_semaphore()

    def greet(**where):
        pl.semaphore_signal(
            barrier, inc=1, device_id=where, device_id_type=pl.DeviceIdType.MESH
        )

    greet(row=me_r + 1 - 2 * core)

    @pl.when(z > 0)
    def _():
        greet(row=me_r - 2)

    @pl.when(z < chips - 1)
    def _():
        greet(row=me_r + 2)

    across = me_r - 1 + 2 * core
    has_across = jnp.logical_and(across >= 0, across < rows)

    @pl.when(has_across)
    def _():
        greet(row=across)

    @pl.loop(1, frames)
    def _(step):
        greet(frame=(me_f + step) % frames)

    pl.semaphore_wait(
        barrier,
        frames
        + (z > 0).astype(jnp.int32)
        + (z < chips - 1).astype(jnp.int32)
        + has_across.astype(jnp.int32),
    )

    def remote(src, dst, send, recv, **where):
        return pltpu.make_async_remote_copy(
            src_ref=src, dst_ref=dst, send_sem=send, recv_sem=recv,
            device_id=where, device_id_type=pl.DeviceIdType.MESH,
        )

    def kv_copy(chip, of_core, c, send, to_row):
        src = 2 * chip + of_core
        return remote(kv.at[src, c], kv.at[src, c], send, kv_recv.at[src, c], row=to_row)

    def go_up(chip, c):
        return kv_copy(chip, core, c, up_send.at[chip], me_r + 2)

    def go_down(chip, c):
        return kv_copy(chip, core, c, dn_send.at[chip], me_r - 2)

    def to_partner(chip, c):
        return kv_copy(chip, core, c, pt_send.at[chip], me_r + 1 - 2 * core)

    def wait_slot(chip, of_core, c):
        kv_copy(chip, of_core, c, up_send.at[chip], me_r + 1 - 2 * core).wait_recv()

    def kt_copy(g, to):
        return remote(ktb.at[g], ktb.at[g], kt_send.at[to], kt_recv.at[g], frame=to)

    def h_copy(g, to, c):
        return remote(hb.at[g, c], hb.at[g, c], h_send.at[to], h_recv.at[g, c], frame=to)

    def halo_copy(side, c):
        return remote(
            mixb.at[1, c], mixb.at[2 - 2 * side, c], halo_send.at[side],
            halo_recv.at[1 - side, c], row=me_r - 1 + 2 * side,
        )

    def lend():
        return remote(qs.at[pl.ds(0, lent)], qh, lend_sem.at[0], lend_sem.at[1], row=mate)

    def give_back(c):
        return remote(oh.at[c], sob.at[c], give_sem.at[c], back_sem.at[c], row=mate)

    for c in range(chunks):
        pltpu.make_async_copy(kv.at[me_r, c], kv.at[me_r, c], ld_kv.at[c]).wait()

        @pl.when(has_down(c))
        def _(c=c):
            go_down(z, c).start()

        @pl.when(has_up(c))
        def _(c=c):
            go_up(z, c).start()

        @pl.when(attends(c))
        def _(c=c):
            to_partner(z, c).start()

    pltpu.make_async_copy(qs, qs, ld_misc.at[2]).wait()
    if lent:
        @pl.when(at_end)
        def _():
            lend().start()

    pltpu.make_async_copy(ktb.at[me_f], ktb.at[me_f], ld_misc.at[0]).wait()

    @pl.loop(me_f + 1, frames)
    def _(to):
        kt_copy(me_f, to).start()

    def relay(d, c):
        @pl.when(jnp.logical_and(z - d >= 0, attends(c)))
        def _():
            wait_slot(z - d, core, c)

            @pl.when(has_up(c))
            def _():
                go_up(z - d, c).start()

            to_partner(z - d, c).start()

        @pl.when(jnp.logical_and(z + d < chips, attends(c)))
        def _():
            wait_slot(z + d, core, c)

            @pl.when(has_down(c))
            def _():
                go_down(z + d, c).start()

            to_partner(z + d, c).start()

    last = jnp.maximum(z, chips - 1 - z)

    @pl.loop(1, last)
    def _(d):
        for c in range(chunks):
            relay(d, c)

    pltpu.make_async_copy(rs, rs, ld_misc.at[3]).wait()

    first_head = lax.broadcasted_iota(jnp.int32, (tokens, LANES), 1) < HEAD_DIM
    keys = rows * tokens

    def attend(blocks, c):
        none = jnp.zeros_like(blocks[0])
        queries = jnp.concatenate(
            [part for q in blocks
             for part in (jnp.where(first_head, q, none), jnp.where(first_head, none, q))],
            axis=0,
        )
        scores = lax.dot_general(
            queries, kv[:, c, 0].reshape(keys, LANES), (((1,), (1,)), ((), ())),
            preferred_element_type=jnp.float32,
        )
        top = jnp.max(scores, axis=1, keepdims=True)
        raised = jnp.exp2((scores - top) * (SCALE * LOG2E))
        denom = jnp.sum(raised, axis=1, keepdims=True)
        both = jnp.dot(
            raised.astype(jnp.bfloat16), kv[:, c, 1].reshape(keys, LANES),
            preferred_element_type=jnp.float32,
        ) / denom
        return [
            jnp.where(
                first_head,
                both[2 * i * tokens : (2 * i + 1) * tokens],
                both[(2 * i + 1) * tokens : (2 * i + 2) * tokens],
            ).astype(jnp.bfloat16)
            for i in range(len(blocks))
        ]

    for c in range(chunks):
        if c == 0:
            relay(last, 0)
        if c + 1 < chunks:
            relay(last, c + 1)

        @pl.when(attends(c))
        def _(c=c):
            @pl.loop(0, chips)
            def _(chip):
                wait_slot(chip, 1 - core, c)

        if c < lent:
            @pl.when(helps)
            def _(c=c):
                if c == 0:
                    lend().wait_recv()
                sob[c], oh[c] = attend([qs[c], qh[c]], c)
                give_back(c).start()

            @pl.when(at_end)
            def _(c=c):
                give_back(c).wait_recv()

            if chips > 4:
                @pl.when(jnp.logical_not(jnp.logical_or(at_end, helps)))
                def _(c=c):
                    sob[c] = attend([qs[c]], c)[0]
        else:
            sob[c] = attend([qs[c]], c)[0]

        hb[me_f, c] = (rs[c].astype(jnp.float32) + sob[c].astype(jnp.float32)).astype(jnp.bfloat16)

        @pl.loop(me_f + 1, frames)
        def _(to, c=c):
            h_copy(me_f, to, c).start()

        pltpu.make_async_copy(sob.at[c], so_hbm.at[0, 0, :, lanes(c)], out_sem.at[0]).start()

    pltpu.make_async_copy(qts, qts, ld_misc.at[1]).wait()

    @pl.loop(0, me_f)
    def _(g):
        kt_copy(g, me_f).wait_recv()

    flat = chunks * tokens
    same = (
        (lax.broadcasted_iota(jnp.int32, (2 * LANES, LANES), 0) // HEAD_DIM) % 2
        == lax.broadcasted_iota(jnp.int32, (2 * LANES, LANES), 1) // HEAD_DIM
    )
    spread = jnp.where(same, 1.0, 0.0).astype(jnp.bfloat16)
    peak[...] = jnp.full(peak.shape, -1e30, jnp.float32)

    @pl.loop(0, me_f + 1)
    def _(g):
        product = (
            qts[...].reshape(flat, LANES).astype(jnp.float32)
            * ktb[g].reshape(flat, LANES).astype(jnp.float32)
        )
        high = product.astype(jnp.bfloat16)
        low = (product - high.astype(jnp.float32)).astype(jnp.bfloat16)
        score = jnp.dot(
            jnp.concatenate([high, low], axis=1), spread, preferred_element_type=jnp.float32
        )
        tsc[g] = score
        peak[...] = jnp.maximum(peak[...], score)

    rden[...] = jnp.zeros(rden.shape, jnp.float32)

    @pl.loop(0, me_f + 1)
    def _(g):
        raised = jnp.exp2((tsc[g] - peak[...]) * (SCALE * LOG2E))
        rden[...] += raised
        wts[g] = raised.astype(jnp.bfloat16)

    rden[...] = 1.0 / rden[...]

    for c in range(chunks):
        @pl.loop(0, me_f)
        def _(g, c=c):
            h_copy(g, me_f, c).wait_recv()

        here = pl.ds(c * tokens, tokens)

        def add(g, total):
            return total + wts[g, here].astype(jnp.float32) * hb[g, c].astype(jnp.float32)

        total = lax.fori_loop(0, me_f + 1, add, jnp.zeros((tokens, LANES), jnp.float32))
        temporal = (total * rden[here]).astype(jnp.bfloat16)
        mixb[1, c] = (
            hb[me_f, c].astype(jnp.float32) + temporal.astype(jnp.float32)
        ).astype(jnp.bfloat16)

        @pl.when(me_r > 0)
        def _(c=c):
            halo_copy(0, c).start()

        @pl.when(me_r < rows - 1)
        def _(c=c):
            halo_copy(1, c).start()

    pltpu.make_async_copy(cwv, cwv, ld_misc.at[4]).wait()
    pltpu.make_async_copy(cbv, cbv, ld_misc.at[5]).wait()

    @pl.when(me_r == 0)
    def _():
        mixb[0] = jnp.zeros(mixb.shape[1:], mixb.dtype)

    @pl.when(me_r == rows - 1)
    def _():
        mixb[2] = jnp.zeros(mixb.shape[1:], mixb.dtype)

    position = lax.broadcasted_iota(jnp.int32, (tokens, LANES), 0)
    for c in range(chunks):
        @pl.when(me_r > 0)
        def _(c=c):
            remote(
                mixb.at[0, c], mixb.at[0, c], halo_send.at[0], halo_recv.at[0, c],
                row=me_r - 1,
            ).wait_recv()

        @pl.when(me_r < rows - 1)
        def _(c=c):
            remote(
                mixb.at[2, c], mixb.at[2, c], halo_send.at[1], halo_recv.at[1, c],
                row=me_r + 1,
            ).wait_recv()

        lines = [mixb[a, c].astype(jnp.float32) for a in range(3)]
        taps = [
            sum(cwv[a, pl.ds(b, 1), lanes(c)] * lines[a] for a in range(3)) for b in range(3)
        ]
        left = jnp.where(position == 0, 0.0, pltpu.roll(taps[0], 1, 0))
        right = jnp.where(position == tokens - 1, 0.0, pltpu.roll(taps[2], tokens - 1, 0))
        conv = cbv[pl.ds(c * LANES, LANES)].reshape(1, LANES) + taps[1] + left + right
        inner = math.sqrt(2.0 / math.pi) * (conv + 0.044715 * (conv * conv * conv))
        bob[c] = (lines[1] + 0.5 * conv * (1.0 + jnp.tanh(inner))).astype(jnp.bfloat16)
        pltpu.make_async_copy(bob.at[c], bo_hbm.at[0, 0, :, lanes(c)], out_sem.at[1]).start()

    def drain(ref, sem):
        pltpu.make_async_copy(ref, ref, sem).wait()

    some = pl.ds(lent, chunks - lent)

    @pl.loop(0, chips)
    def _(chip):
        src = 2 * chip + core

        @pl.when(at_end)
        def _():
            drain(kv.at[src, some], pt_send.at[chip])

        @pl.when(jnp.logical_not(at_end))
        def _():
            drain(kv.at[src], pt_send.at[chip])

    bound = 1 if lent else 0

    @pl.loop(0, z + 1)
    def _(chip):
        @pl.when(z < chips - 1 - bound)
        def _():
            drain(kv.at[2 * chip + core], up_send.at[chip])

        @pl.when(jnp.logical_and(z < chips - 1, z >= chips - 1 - bound))
        def _():
            drain(kv.at[2 * chip + core, some], up_send.at[chip])

    @pl.loop(z, chips)
    def _(chip):
        @pl.when(z > bound)
        def _():
            drain(kv.at[2 * chip + core], dn_send.at[chip])

        @pl.when(jnp.logical_and(z > 0, z <= bound))
        def _():
            drain(kv.at[2 * chip + core, some], dn_send.at[chip])

    @pl.loop(me_f + 1, frames)
    def _(to):
        kt_copy(me_f, to).wait_send()
        drain(hb.at[me_f], h_send.at[to])

    @pl.when(me_r > 0)
    def _():
        drain(mixb.at[1], halo_send.at[0])

    @pl.when(me_r < rows - 1)
    def _():
        drain(mixb.at[1], halo_send.at[1])

    if lent:
        @pl.when(at_end)
        def _():
            lend().wait_send()

    for c in range(lent):
        @pl.when(helps)
        def _(c=c):
            give_back(c).wait_send()

    pltpu.make_async_copy(sob, sob, out_sem.at[0]).wait()
    pltpu.make_async_copy(bob, bob, out_sem.at[1]).wait()


def on_device(frames, rows, *args):
    block = args[0]
    _, _, tokens, channels = block.shape
    chunks = channels // LANES
    chips = rows // 2
    lent = chunks * 3 // 6 if chips >= 4 else 0
    held = max(lent, 1)
    slab = (chunks, tokens, LANES)
    flat = (chunks * tokens, LANES)
    bf16, f32 = jnp.bfloat16, jnp.float32
    dma = pltpu.SemaphoreType.DMA
    anywhere = pl.BlockSpec(memory_space=pl.ANY)
    return pl.pallas_call(
        functools.partial(block_kernel, frames, rows, chunks, tokens, lent),
        out_shape=(jax.ShapeDtypeStruct(block.shape, bf16),) * 2,
        in_specs=[anywhere] * 8,
        out_specs=(anywhere, anywhere),
        scratch_shapes=[
            pltpu.VMEM((rows, chunks, 2, tokens, LANES), bf16),
            pltpu.VMEM(slab, bf16),
            pltpu.VMEM((held,) + slab[1:], bf16),
            pltpu.VMEM((held,) + slab[1:], bf16),
            pltpu.VMEM(slab, bf16),
            pltpu.VMEM(slab, bf16),
            pltpu.VMEM((frames,) + slab, bf16),
            pltpu.VMEM((frames,) + slab, bf16),
            pltpu.VMEM((frames,) + flat, f32),
            pltpu.VMEM((frames,) + flat, bf16),
            pltpu.VMEM(flat, f32),
            pltpu.VMEM(flat, f32),
            pltpu.VMEM((3,) + slab, bf16),
            pltpu.VMEM(slab, bf16),
            pltpu.VMEM(slab, bf16),
            pltpu.VMEM(args[6].shape, f32),
            pltpu.VMEM(args[7].shape, f32),
            dma((chunks,)), dma((6,)), dma((rows, chunks)),
            dma((chips,)), dma((chips,)), dma((chips,)),
            dma((frames,)), dma((frames,)), dma((frames, chunks)), dma((frames,)),
            dma((2, chunks)), dma((2,)), dma((2,)),
            dma((2,)), dma((held,)), dma((held,)),
        ],
        compiler_params=pltpu.CompilerParams(collective_id=0, has_side_effects=True,
            vmem_limit_bytes=(14 << 20) + (rows << 18) + (frames << 19)),
        name="block",
    )(*[pltpu.with_memory_space_constraint(a, pltpu.HBM) for a in args])


def solution(mesh):
    split = P("frame", "row", None, None)
    return jax.shard_map(
        functools.partial(on_device, mesh.shape["frame"], mesh.shape["row"]),
        mesh=mesh,
        in_specs=(split,) * 6 + (P(), P()),
        out_specs=(split, split),
        check_vma=False,
    )
```
